32 devices in a mesh: ctx: 16 (over z, y, x), head: 2 (over core).
Axes of the slice: x: 2, y: 2, z: 4, core: 2. Of those that a mesh axis runs over, the one named last changes fastest.
Arguments:
- queries: bfloat16 [2, 4096, 4096], P(None, 'ctx', 'head'), may hold values from -6 to 6
- keys: bfloat16 [2, 4096, 4096], P(None, 'ctx', 'head'), may hold values from -6 to 6
- values: bfloat16 [2, 4096, 4096], P(None, 'ctx', 'head'), may hold values from -6 to 6
- token_gate: float32 [2, 32, 4096], P(None, 'head', 'ctx'), may hold values from 0.2 to 1
- head_rate: float32 [32], P('head'), may hold values from 5.722046e-07 to 0.001953125
- init_state: float32 [32, 128, 128], P('head'), may hold values from -0.53033006 to 0.53033006
- norm_gain: float32 [4096], P('head'), may hold values from 0.5 to 1.5
- out_proj: bfloat16 [4096, 4096], P('head'), may hold values from -0.09375 to 0.09375
- plan: int32 [2], replicated, may hold values from 0 to 1, each once
Outputs:
- layer_out: bfloat16 [4096, 2, 4096], P(('ctx', 'head'))
The draws below stay inside these ranges and needn't reach their ends.
Inputs may be any that keep to these rules, and one draw needn't show every extreme that they name: `plan`: each sequence appears exactly once.
All inputs are finite; a program needn't handle non-finite values.
Results may differ from the reference program's by a relative error of at most 0.0049.
Values sent between devices are 32-bit elements; how exact they have to be, the bound alone decides.
No kernel may reach another device: no remote copies, remote signals or barrier semaphores. Data moves between devices by JAX's collectives and lax.ppermute only.
A program may use at most 128 MiB of HBM per device.

```python
import math
import jax
import jax.numpy as jnp
from jax import lax

D = 4096
HEADS = 32
HS = 128
MB = 64
SEQS = 2
TOKENS = 4096


def level_of(stream_key, dims, cuts, smallest, largest):
    def one(dim, shards_of):
        steps = jax.random.uniform(jax.random.fold_in(jax.random.fold_in(stream_key, 6), dim), (shards_of,), jnp.float32, smallest / len(cuts), largest / len(cuts))
        return jnp.repeat(jnp.exp(steps), dims[dim] // shards_of).reshape((-1,) + (1,) * (len(dims) - dim - 1))

    level = one(*cuts[0])
    for cut in cuts[1:]:
        level = level * one(*cut)
    return level


def normal_values(rng, dims, width, most, cuts=(), held_as=jnp.bfloat16):
    level = level_of(rng, dims, cuts, -0.22, 0.18) if cuts else 1.0
    drawn = jax.random.normal(rng, dims, jnp.float32) * width * level
    return jnp.minimum(jnp.maximum(drawn, -most), most).astype(held_as)


def setup_inputs(seed: int = 0) -> dict:
    arg_keys = jax.random.split(jax.random.key(seed), 10)
    queries = normal_values(arg_keys[0], (SEQS, TOKENS, HEADS * HS), 1.0, 6.0, ((1, 16), (2, 2)))
    keys = normal_values(arg_keys[1], (SEQS, TOKENS, HEADS * HS), 1.0, 6.0, ((1, 16), (2, 2)))
    values = normal_values(arg_keys[2], (SEQS, TOKENS, HEADS * HS), 1.0, 6.0, ((1, 16), (2, 2)))
    token_gate = jnp.clip(0.2 + 0.8 * jax.random.uniform(arg_keys[3], (SEQS, HEADS, TOKENS), jnp.float32) ** level_of(arg_keys[3], (SEQS, HEADS, TOKENS), ((1, 2), (2, 16)), -0.2, 0.2), 0.2, 1.0)
    head_rate = jnp.clip(jnp.exp(math.log(0.001953125) - 8.135445 * jax.random.uniform(arg_keys[4], (HEADS,), jnp.float32) ** level_of(arg_keys[4], (HEADS,), ((0, 2),), -0.2, 0.2)), 5.722046125811175e-07, 0.001953125)
    init_state = normal_values(arg_keys[5], (HEADS, HS, HS), (HS ** -0.5), 0.53033006, ((0, 2),), jnp.float32)
    norm_gain = jnp.clip(1.0 + 0.1 * jax.random.normal(arg_keys[6], (HEADS * HS,), jnp.float32), 0.5, 1.5)
    out_proj = normal_values(arg_keys[7], (HEADS * HS, D), (HEADS * HS) ** -0.5, 0.09375, ((0, 2),))
    plan = jax.random.permutation(arg_keys[8], SEQS).astype(jnp.int32)
    return {"queries": queries, "keys": keys, "values": values, "token_gate": token_gate, "head_rate": head_rate, "init_state": init_state, "norm_gain": norm_gain, "out_proj": out_proj, "plan": plan}


EPS = 1e-06

def run_sequence(qs, ks, vs, eta, start):
    best = lax.Precision.HIGHEST
    blocks = TOKENS // MB

    def split(arr):
        arr = arr.astype(jnp.float32).reshape(blocks, MB, HEADS, HS)
        return jnp.transpose(arr, (0, 2, 1, 3))
    qb, kb, vb = (split(qs), split(ks), split(vs))
    eb = jnp.transpose(eta.reshape(HEADS, blocks, MB), (1, 0, 2))
    lower = jnp.arange(MB)[:, None] >= jnp.arange(MB)[None, :]

    def step(weights, blk):
        qm, km, vm, em = blk
        err = jnp.einsum('hmi,hij->hmj', km, weights, precision=best) - vm
        qw = jnp.einsum('hmi,hij->hmj', qm, weights, precision=best)
        scores = jnp.einsum('hmi,hni->hmn', qm, km, precision=best) * em[:, None, :]
        scores = jnp.where(lower[None], scores, 0.0)
        zout = qw - jnp.einsum('hmn,hnj->hmj', scores, err, precision=best)
        weights = weights - jnp.einsum('hmi,hmj->hij', km * em[..., None], err, precision=best)
        return (weights, zout)
    _, zall = lax.scan(step, start, (qb, kb, vb, eb))
    return jnp.transpose(zall, (0, 2, 1, 3)).reshape(TOKENS, HEADS, HS)

def reference(queries, keys, values, token_gate, head_rate, init_state, norm_gain, out_proj, plan):
    gain = norm_gain.reshape(HEADS, HS)
    outputs = []
    for step_index in range(SEQS):
        seq = plan[step_index]
        eta = token_gate[seq] * head_rate[:, None]
        zvals = run_sequence(queries[seq], keys[seq], values[seq], eta, init_state)
        scale = lax.rsqrt(lax.optimization_barrier(jnp.mean(zvals * zvals, axis=-1, keepdims=True)) + EPS)
        normed = (zvals * scale * gain[None]).astype(jnp.bfloat16).reshape(TOKENS, HEADS * HS)
        outputs.append(jnp.dot(normed, out_proj, preferred_element_type=jnp.float32).astype(jnp.bfloat16))
    return jnp.stack(outputs, axis=1)
```

```python
import functools

import jax
import jax.numpy as jnp
from jax import lax
from jax.experimental import pallas as pl
from jax.experimental.pallas import tpu as pltpu
from jax.sharding import PartitionSpec as P

HS = 128
MB = 64
EPS = 1e-06
F32 = jnp.float32
BF16 = jnp.bfloat16


def split2(x):
    hi = x.astype(BF16)
    return hi, (x - hi.astype(F32)).astype(BF16)


def mm(a, b, dims=((1,), (0,))):
    return lax.dot_general(a, b, (dims, ((), ())), preferred_element_type=F32)


def mm3(a, b):
    (ah, al), (bh, bl) = a, b
    return mm(ah, bh) + (mm(al, bh) + mm(ah, bl))


def cat2(pairs, axis):
    return tuple(jnp.concatenate(part, axis=axis) for part in zip(*pairs))


def eta_row(gate_ref, rate_ref, head):
    return gate_ref[0, pl.ds(head, 1), :] * rate_ref[head]


def maps_kernel(heads_step, plan_ref, k_ref, v_ref, gate_ref, rate_ref, map_ref, thi_ref, tlo_ref):
    rows = k_ref.shape[1]
    for h in range(heads_step):
        eta = eta_row(gate_ref, rate_ref, pl.program_id(0) * heads_step + h)
        cols = slice(h * HS, (h + 1) * HS)
        k = k_ref[0, :, cols]
        first = jnp.concatenate([k.astype(F32), -v_ref[0, :, cols].astype(F32)], axis=1)
        done = []
        for m in range(rows // MB):
            at = slice(m * MB, (m + 1) * MB)
            block = first[at]
            if m:
                near = mm(k[at], k[: m * MB], ((1,), (1,))) * eta[:, : m * MB]
                block = block - mm3(split2(near), cat2(done, 0))
            done.append(split2(block))
        whole = cat2(done, 0)
        weighted = jnp.transpose(k.astype(F32)) * eta
        total = mm3(split2(weighted), whole)
        map_ref[h, 0] = total[:, :HS]
        map_ref[h, 1] = -total[:, HS:]
        thi_ref[h] = whole[0]
        tlo_ref[h] = whole[1]


def reads_kernel(heads_step, plan_ref, q_ref, k_ref, gate_ref, rate_ref, thi_ref, tlo_ref, phi_ref, plo_ref, rest_ref):
    rows = q_ref.shape[1]
    lower = lax.broadcasted_iota(jnp.int32, (rows, rows), 0) >= lax.broadcasted_iota(jnp.int32, (rows, rows), 1)
    for h in range(heads_step):
        eta = eta_row(gate_ref, rate_ref, pl.program_id(0) * heads_step + h)
        cols = slice(h * HS, (h + 1) * HS)
        q = q_ref[0, :, cols]
        scores = mm(q, k_ref[0, :, cols], ((1,), (1,))) * eta
        scores = jnp.where(lower, scores, 0.0)
        taken = mm3(split2(scores), (thi_ref[h], tlo_ref[h]))
        hi, lo = split2(q.astype(F32) - taken[:, :HS])
        phi_ref[:, cols] = hi
        plo_ref[:, cols] = lo
        rest_ref[:, cols] = -taken[:, HS:]


def chain_kernel(all_out, info_ref, map_ref, start_ref, moved_ref, out_ref):
    members, per = map_ref.shape[:2]
    is_first = info_ref[1] == 0
    states = [jnp.where(is_first, start_ref[u], moved_ref[u]) for u in range(per)]
    for m in range(members):
        for u in range(per):
            if all_out:
                out_ref[m, u] = states[u]
            if all_out and m == members - 1:
                continue
            pulled = mm3(split2(map_ref[m, u, 0]), split2(states[u]))
            states[u] = states[u] - pulled + map_ref[m, u, 1]
    if not all_out:
        for u in range(per):
            out_ref[u] = states[u]


def final_kernel(heads, parts, me_ref, phi_ref, plo_ref, rest_ref, state_ref, gain_ref, proj_ref, *refs):
    outs, normed = refs[:-1], refs[-1]

    @pl.when(pl.program_id(0) == 0)
    def _():
        for h in range(heads):
            cols = slice(h * HS, (h + 1) * HS)
            z = mm3((phi_ref[:, cols], plo_ref[:, cols]), split2(state_ref[h])) + rest_ref[:, cols]
            scale = lax.rsqrt(jnp.mean(z * z, axis=-1, keepdims=True) + EPS)
            normed[:, cols] = (z * scale * gain_ref[:, cols]).astype(BF16)

    piece = normed.shape[0] // parts
    for d in range(parts):
        begin = pl.multiple_of((me_ref[0] ^ d) * piece, piece)
        outs[d][...] = mm(normed[pl.ds(begin, piece), :], proj_ref[...])


def cost(flops, nbytes):
    return pl.CostEstimate(flops=int(flops), bytes_accessed=int(nbytes), transcendentals=0)


def per_device(queries, keys, values, token_gate, head_rate, init_state, norm_gain, out_proj, plan):
    seqs, rows, width = queries.shape
    heads = init_state.shape[0]
    model = out_proj.shape[1]
    ctx, parts = lax.axis_size("ctx"), lax.axis_size("head")
    group = 1
    while group < 8 and heads % (2 * group) == 0 and ctx % (2 * group) == 0:
        group *= 2
    per = heads // group
    groups = [list(range(g, g + group)) for g in range(0, ctx, group)]
    onward = [(i, i + group) for i in range(ctx - group)]
    position = lax.axis_index("ctx")
    info = jnp.stack([lax.rem(position, group), lax.div(position, group)]).astype(jnp.int32)
    me = lax.axis_index("head").astype(jnp.int32).reshape(1)
    step = 4 if heads % 4 == 0 else 1
    smem = pl.BlockSpec(memory_space=pltpu.SMEM)

    def seq_block(s):
        return pl.BlockSpec((1, rows, step * HS), lambda i, plan_ref: (plan_ref[s], 0, i))

    def gate_block(s):
        return pl.BlockSpec((1, heads, rows), lambda i, plan_ref: (plan_ref[s], 0, 0))

    t_block = pl.BlockSpec((step, rows, 2 * HS), lambda i, plan_ref: (i, 0, 0))
    col_block = pl.BlockSpec((rows, step * HS), lambda i, plan_ref: (0, i))

    def maps_of(s):
        return pl.pallas_call(
            functools.partial(maps_kernel, step),
            grid_spec=pltpu.PrefetchScalarGridSpec(
                num_scalar_prefetch=1,
                grid=(heads // step,),
                in_specs=[seq_block(s), seq_block(s), gate_block(s), smem],
                out_specs=[
                    pl.BlockSpec((step, 2, HS, HS), lambda i, plan_ref: (i, 0, 0, 0)),
                    t_block,
                    t_block,
                ],
            ),
            out_shape=[
                jax.ShapeDtypeStruct((heads, 2, HS, HS), F32),
                jax.ShapeDtypeStruct((heads, rows, 2 * HS), BF16),
                jax.ShapeDtypeStruct((heads, rows, 2 * HS), BF16),
            ],
            cost_estimate=cost(heads * 6 * rows * 256 * 256, heads * rows * HS * 12),
            name="maps",
        )(plan, keys, values, token_gate, head_rate)

    def reads_of(s, thi, tlo):
        return pl.pallas_call(
            functools.partial(reads_kernel, step),
            grid_spec=pltpu.PrefetchScalarGridSpec(
                num_scalar_prefetch=1,
                grid=(heads // step,),
                in_specs=[seq_block(s), seq_block(s), gate_block(s), smem, t_block, t_block],
                out_specs=[col_block, col_block, col_block],
            ),
            out_shape=[
                jax.ShapeDtypeStruct((rows, width), BF16),
                jax.ShapeDtypeStruct((rows, width), BF16),
                jax.ShapeDtypeStruct((rows, width), F32),
            ],
            cost_estimate=cost(heads * 8 * rows * 256 * 256, heads * rows * HS * 20),
            name="reads",
        )(plan, queries, keys, token_gate, head_rate, thi, tlo)

    def chain(gathered, moved, all_out):
        members = gathered.shape[0]
        shape = (members, per, HS, HS) if all_out else (per, HS, HS)
        return pl.pallas_call(
            functools.partial(chain_kernel, all_out),
            grid_spec=pltpu.PrefetchScalarGridSpec(
                num_scalar_prefetch=1,
                grid=(1,),
                in_specs=[
                    pl.BlockSpec((members, per, 2, HS, HS), lambda i, info_ref: (0, 0, 0, 0, 0)),
                    pl.BlockSpec((per, HS, HS), lambda i, info_ref: (info_ref[0], 0, 0)),
                    pl.BlockSpec((per, HS, HS), lambda i, info_ref: (0, 0, 0)),
                ],
                out_specs=pl.BlockSpec(shape, lambda i, info_ref: (0,) * len(shape)),
            ),
            out_shape=jax.ShapeDtypeStruct(shape, F32),
            cost_estimate=cost(members * per * 6 * HS**3, members * per * HS * HS * 12),
            name="chain",
        )(info, gathered, init_state, moved)

    wide = 512 if model % 512 == 0 else model

    def final_of(reads, state):
        phi, plo, rest = reads
        full = lambda i, me_ref: (0, 0)
        piece = rows // parts
        return pl.pallas_call(
            functools.partial(final_kernel, heads, parts),
            grid_spec=pltpu.PrefetchScalarGridSpec(
                num_scalar_prefetch=1,
                grid=(model // wide,),
                in_specs=[
                    pl.BlockSpec((rows, width), full),
                    pl.BlockSpec((rows, width), full),
                    pl.BlockSpec((rows, width), full),
                    pl.BlockSpec((heads, HS, HS), lambda i, me_ref: (0, 0, 0)),
                    pl.BlockSpec((1, width), full),
                    pl.BlockSpec((width, wide), lambda i, me_ref: (0, i)),
                ],
                out_specs=[pl.BlockSpec((piece, wide), lambda i, me_ref: (0, i))] * parts,
                scratch_shapes=[pltpu.VMEM((rows, width), BF16)],
            ),
            out_shape=[jax.ShapeDtypeStruct((piece, model), F32)] * parts,
            cost_estimate=cost(2 * rows * width * model, 2 * width * model + 4 * rows * model),
            name="final",
        )(me, phi, plo, rest, state, norm_gain.reshape(1, width), out_proj)

    def shared(block):
        if group == 1:
            return block
        return lax.all_to_all(block, "ctx", 0, 0, axis_index_groups=groups)

    mapped = [maps_of(s) for s in range(seqs)]
    gathered = [shared(maps.reshape(group, per, 2, HS, HS)) for maps, _, _ in mapped]
    reads = [reads_of(s, thi, tlo) for s, (_, thi, tlo) in enumerate(mapped)]
    outs = []
    for s in range(seqs):
        moved = jnp.zeros((per, HS, HS), F32)
        for _ in range(ctx // group - 1):
            moved = lax.ppermute(chain(gathered[s], moved, False), "ctx", onward)
        entering = shared(chain(gathered[s], moved, True)).reshape(heads, HS, HS)
        products = final_of(reads[s], entering)
        total = products[0]
        for d in range(1, parts):
            total = total + lax.ppermute(products[d], "head", [(i, i ^ d) for i in range(parts)])
        outs.append(total)
    return jnp.stack(outs, axis=1).astype(BF16)


def solution(mesh):
    return jax.shard_map(
        per_device,
        mesh=mesh,
        in_specs=(
            P(None, "ctx", "head"),
            P(None, "ctx", "head"),
            P(None, "ctx", "head"),
            P(None, "head", "ctx"),
            P("head"),
            P("head", None, None),
            P("head"),
            P("head", None),
            P(),
        ),
        out_specs=P(("ctx", "head"), None, None),
        check_vma=False,
    )
```

```python
import functools

import jax
import jax.numpy as jnp
from jax import lax
from jax.experimental import pallas as pl
from jax.experimental.pallas import tpu as pltpu
from jax.sharding import PartitionSpec as P


HS = 128
MB = 64
EPS = 1e-06
STEP = 8
WIDE = 512
SMALL = 14
LARGE = 30
UP_PERMUTE = (False, True)
DOWN_PERMUTE = (False, True)
F32 = jnp.float32
BF16 = jnp.bfloat16


def mm(a, b, dims=((1,), (0,))):
    return lax.dot_general(a, b, (dims, ((), ())), preferred_element_type=F32)


ROWS_BY_ROWS = ((1,), (1,))


def iotas(rows, cols):
    return tuple(lax.broadcasted_iota(jnp.int32, (rows, cols), axis) for axis in (0, 1))


def eta_rows(gate_ref, rate_ref, heads_step, sign):
    first = pl.program_id(0) * heads_step
    return [gate_ref[0, pl.ds(first + h, 1), :] * (sign * rate_ref[first + h]) for h in range(heads_step)]


def maps_kernel(heads_step, per, plan_ref, rot_ref, k_ref, v_ref, gate_ref, rate_ref, map_ref, t_ref):
    rows = k_ref.shape[1]
    pair = 2 * MB
    each = range(heads_step)
    etas = eta_rows(gate_ref, rate_ref, heads_step, 1.0)
    to, of = iotas(MB, pair)
    left, diag = of < MB, of == to + MB
    eye = jnp.where(jnp.equal(*iotas(pair, pair)), 1.0, 0.0).astype(BF16)
    ks = [k_ref[0, :, h * HS : (h + 1) * HS] for h in each]
    for h in each:
        t_ref[h] = jnp.concatenate([ks[h], -v_ref[0, :, h * HS : (h + 1) * HS]], axis=1)
    for begin in range(0, rows, pair):
        end, late = begin + pair, begin + MB
        if begin:
            reach = [-mm(ks[h][begin:end], ks[h][:begin], ROWS_BY_ROWS) * etas[h][:, :begin] for h in each]
            reach = [jnp.concatenate([r.astype(BF16), eye], axis=1) for r in reach]
            for h in each:
                t_ref[h, begin:end] = mm(reach[h], t_ref[h, :end]).astype(BF16)
        near = [-mm(ks[h][late:end], ks[h][begin:end], ROWS_BY_ROWS) * etas[h][:, begin:end] for h in each]
        near = [jnp.where(left, n, jnp.where(diag, 1.0, 0.0)).astype(BF16) for n in near]
        for h in each:
            t_ref[h, late:end] = mm(near[h], t_ref[h, begin:end]).astype(BF16)
    weighted = [(jnp.transpose(ks[h].astype(F32)) * etas[h]).astype(BF16) for h in each]
    for h in each:
        total = mm(weighted[h], t_ref[h])
        place = lax.rem(rot_ref[0], heads_step // per) ^ (h // per)
        map_ref[place, h % per, 0] = total[:, :HS]
        map_ref[place, h % per, 1] = total[:, HS:]


def reads_kernel(heads_step, plan_ref, q_ref, k_ref, gate_ref, rate_ref, t_ref, less_ref, rest_ref):
    rows = q_ref.shape[1]
    pair = 2 * MB
    each = range(heads_step)
    etas = eta_rows(gate_ref, rate_ref, heads_step, -1.0)
    lower = jnp.greater_equal(*iotas(pair, pair))
    for begin in range(0, rows, pair):
        end = begin + pair
        scores = []
        for h in each:
            cols = slice(h * HS, (h + 1) * HS)
            score = mm(q_ref[0, begin:end, cols], k_ref[0, :end, cols], ROWS_BY_ROWS) * etas[h][:, :end]
            parts = [score[:, :begin]] if begin else []
            parts.append(jnp.where(lower, score[:, begin:], 0.0))
            scores.append(jnp.concatenate(parts, axis=1).astype(BF16))
        for h in each:
            cols = slice(h * HS, (h + 1) * HS)
            taken = mm(scores[h], t_ref[h, :end])
            less_ref[begin:end, cols] = taken[:, :HS].astype(BF16)
            rest_ref[begin:end, cols] = taken[:, HS:]


def advance(state, both):
    return state - mm(both[0].astype(BF16), state.astype(BF16)) - both[1]


def chain_kernel(group, hops, all_out, info_ref, *refs):
    maps, (start_ref, moved_ref), out_ref, held = refs[:group], refs[group:-2], refs[-2], refs[-1]
    rot = info_ref[0]
    for d in range(group):
        held[d ^ rot] = maps[d][0]
    per = held.shape[1]
    states = [start_ref[u] for u in range(per)]
    if hops:
        states = [jnp.where(info_ref[1] == 0, states[u], moved_ref[u]) for u in range(per)]
    for m in range(group):
        for u in range(per):
            if all_out:
                out_ref[m ^ info_ref[3], u] = states[u]
            if not all_out or m < group - 1:
                states[u] = advance(states[u], held[m, u])
    if not all_out:
        for u in range(per):
            out_ref[u] = states[u]


def final_kernel(steps, parts, group, plan_ref, me_ref, rot_ref, q_ref, less_ref, rest_ref, gain_ref, proj_ref, *refs):
    states, outs, (held, normed, proj, sems) = refs[:group], refs[group:-4], refs[-4:]
    piece = normed.shape[1] // parts
    i = pl.program_id(0)
    per = held.shape[1]

    wide = proj.shape[3]

    def chunk(c):
        part = proj_ref.at[:, :, pl.ds(pl.multiple_of(c * wide, wide), wide)]
        return pltpu.make_async_copy(part, proj.at[c], sems.at[c])

    @pl.when(i == 0)
    def _():
        for c in range(proj.shape[0]):
            chunk(c).start()
        for d in range(group):
            held[d ^ rot_ref[0]] = states[d][0]

    @pl.when(i < steps)
    def _():
        heads_step = normed.shape[2] // HS
        zs = []
        for h in range(heads_step):
            cols = slice(h * HS, (h + 1) * HS)
            state = held[i * (heads_step // per) + h // per, h % per]
            main = state.astype(BF16)
            small = (state - main.astype(F32)).astype(BF16)
            q = q_ref[0, :, cols]
            z = mm(jnp.concatenate([q, less_ref[:, cols]], axis=1), jnp.concatenate([main, main], axis=0))
            zs.append(z + mm(q, small) + rest_ref[:, cols])
        for h in range(heads_step):
            cols = slice(h * HS, (h + 1) * HS)
            scale = lax.rsqrt(jnp.mean(zs[h] * zs[h], axis=-1, keepdims=True) + EPS)
            out = (zs[h] * scale * gain_ref[:, cols]).astype(BF16)
            for p in range(parts):
                begin = pl.multiple_of((me_ref[0] ^ p) * piece, piece)
                normed[i, pl.ds(begin, piece), cols] = out[p * piece : (p + 1) * piece]

    @pl.when(i >= steps)
    def _():
        chunk(i - steps).wait()
        product = sum(mm(normed[n], proj[i - steps, n]) for n in range(steps))
        for d in range(parts):
            outs[d][...] = product[d * piece : (d + 1) * piece]


def in_hbm(x):
    return pltpu.with_memory_space_constraint(x, pltpu.HBM)


def in_vmem(x):
    return pltpu.with_memory_space_constraint(x, pltpu.VMEM)


def limit(mib):
    return pltpu.CompilerParams(vmem_limit_bytes=mib * 2**20)


def cost(flops, nbytes):
    return pl.CostEstimate(flops=int(flops), bytes_accessed=int(nbytes), transcendentals=0)


def per_device(queries, keys, values, token_gate, head_rate, init_state, norm_gain, out_proj, plan):
    seqs, rows, width = queries.shape
    heads = init_state.shape[0]
    model = out_proj.shape[1]
    ctx, parts = lax.axis_size("ctx"), lax.axis_size("head")
    plan, head_rate = in_hbm(plan), in_hbm(head_rate)
    group = 1
    while group < 8 and heads % (2 * group) == 0 and ctx % (2 * group) == 0:
        group *= 2
    per = heads // group
    groups = [list(range(g, g + group)) for g in range(0, ctx, group)]
    onward = [(i, i + group) for i in range(ctx - group)]
    position = lax.axis_index("ctx").astype(jnp.int32)
    place, block = lax.rem(position, group), lax.div(position, group)
    rots = {True: place.reshape(1), False: jnp.zeros((1,), jnp.int32)}
    me = lax.axis_index("head").astype(jnp.int32).reshape(1)
    step = STEP if heads % STEP == 0 else heads
    smem = pl.BlockSpec(memory_space=pltpu.SMEM)

    def seq_block(s):
        return pl.BlockSpec((1, rows, step * HS), lambda i, plan_ref: (plan_ref[s], 0, i))

    def gate_block(s):
        return pl.BlockSpec((1, heads, rows), lambda i, plan_ref: (plan_ref[s], 0, 0))

    t_block = pl.BlockSpec((step, rows, 2 * HS), lambda i, plan_ref: (i, 0, 0))
    col_block = pl.BlockSpec((rows, step * HS), lambda i, plan_ref: (0, i))

    def maps_of(s):
        part = step // per
        grid_spec = pltpu.PrefetchScalarGridSpec(
            num_scalar_prefetch=2,
            grid=(heads // step,),
            in_specs=[
                pl.BlockSpec((1, rows, step * HS), lambda i, plan_ref, rot_ref: (plan_ref[s], 0, i)),
                pl.BlockSpec((1, rows, step * HS), lambda i, plan_ref, rot_ref: (plan_ref[s], 0, i)),
                pl.BlockSpec((1, heads, rows), lambda i, plan_ref, rot_ref: (plan_ref[s], 0, 0)),
                smem,
            ],
            out_specs=[
                pl.BlockSpec(
                    (part, per, 2, HS, HS),
                    lambda i, plan_ref, rot_ref: (lax.div(rot_ref[0], part) ^ i, 0, 0, 0, 0),
                ),
                pl.BlockSpec((step, rows, 2 * HS), lambda i, plan_ref, rot_ref: (i, 0, 0)),
            ],
        )
        return pl.pallas_call(
            functools.partial(maps_kernel, step, per),
            grid_spec=grid_spec,
            out_shape=[
                (pltpu.VMEM if UP_PERMUTE[s] else pltpu.HBM)((group, per, 2, HS, HS), F32),
                pltpu.HBM((heads, rows, 2 * HS), BF16),
            ],
            cost_estimate=cost(heads * 6 * rows * 256 * 256, heads * rows * HS * 12),
            compiler_params=limit(SMALL),
        )(plan, rots[UP_PERMUTE[s]], in_hbm(keys), in_hbm(values), in_hbm(token_gate), head_rate)

    def reads_of(s, errors):
        return pl.pallas_call(
            functools.partial(reads_kernel, step),
            grid_spec=pltpu.PrefetchScalarGridSpec(
                num_scalar_prefetch=1,
                grid=(heads // step,),
                in_specs=[seq_block(s), seq_block(s), gate_block(s), smem, t_block],
                out_specs=[col_block, col_block],
            ),
            out_shape=[
                pltpu.HBM((rows, width), BF16),
                pltpu.HBM((rows, width), F32),
            ],
            cost_estimate=cost(heads * 8 * rows * 256 * 256, heads * rows * HS * 16),
            compiler_params=limit(SMALL),
        )(plan, in_hbm(queries), in_hbm(keys), in_hbm(token_gate), head_rate, in_hbm(errors))

    def one_of(parts_d, blocks):
        tail = (0,) * (len(blocks) - 1)
        if isinstance(parts_d, list):
            return parts_d, [pl.BlockSpec(blocks, lambda i, *_: (0,) + tail) for _ in parts_d]
        return [parts_d] * group, [pl.BlockSpec(blocks, lambda i, *_, d=d: (d,) + tail) for d in range(group)]

    def chain(s, gathered, moved, all_out):
        shape = (group, per, HS, HS) if all_out else (per, HS, HS)
        info = jnp.concatenate([rots[UP_PERMUTE[s]], block.reshape(1), place.reshape(1), rots[DOWN_PERMUTE[s]]])
        given, map_specs = one_of(gathered, (1, per, 2, HS, HS))
        hops = moved is not None
        return pl.pallas_call(
            functools.partial(chain_kernel, group, hops, all_out),
            grid_spec=pltpu.PrefetchScalarGridSpec(
                num_scalar_prefetch=1,
                grid=(1,),
                in_specs=map_specs
                + [
                    pl.BlockSpec((per, HS, HS), lambda i, info_ref: (info_ref[2], 0, 0)),
                    pl.BlockSpec((per, HS, HS), lambda i, info_ref: (0, 0, 0)),
                ],
                out_specs=pl.BlockSpec(shape, lambda i, info_ref: (0,) * len(shape)),
                scratch_shapes=[pltpu.VMEM((group, per, 2, HS, HS), F32)],
            ),
            out_shape=(pltpu.HBM if all_out and not DOWN_PERMUTE[s] else pltpu.VMEM)(shape, F32),
            compiler_params=limit(SMALL),
            cost_estimate=cost(group * per * 6 * HS**3, group * per * HS * HS * 12),
        )(info, *map(in_vmem, given), in_hbm(init_state), in_vmem(moved) if hops else in_hbm(init_state))

    wide = WIDE if model % WIDE == 0 else model
    steps = heads // step

    def final_of(s, reads, entering):
        less, rest = reads
        piece = rows // parts
        early = lambda i: jnp.minimum(i, steps - 1)
        late = lambda i: jnp.maximum(i - steps, 0)
        by_cols = pl.BlockSpec((rows, step * HS), lambda i, *_: (0, early(i)))
        given, state_specs = one_of(entering, (1, per, HS, HS))
        return pl.pallas_call(
            functools.partial(final_kernel, steps, parts, group),
            grid_spec=pltpu.PrefetchScalarGridSpec(
                num_scalar_prefetch=3,
                grid=(steps + model // wide,),
                in_specs=[
                    pl.BlockSpec((1, rows, step * HS), lambda i, plan_ref, *_: (plan_ref[s], 0, early(i))),
                    by_cols,
                    by_cols,
                    pl.BlockSpec((1, step * HS), lambda i, *_: (0, early(i))),
                    pl.BlockSpec(memory_space=pltpu.HBM),
                ]
                + state_specs,
                out_specs=[pl.BlockSpec((piece, wide), lambda i, *_: (0, late(i)))] * parts,
                scratch_shapes=[
                    pltpu.VMEM((group, per, HS, HS), F32),
                    pltpu.VMEM((steps, rows, step * HS), BF16),
                    pltpu.VMEM((model // wide, steps, step * HS, wide), BF16),
                    pltpu.SemaphoreType.DMA((model // wide,)),
                ],
            ),
            compiler_params=limit(LARGE),
            out_shape=[jax.ShapeDtypeStruct((piece, model), F32)] * parts,
            cost_estimate=cost(2 * rows * width * model, 2 * width * model + 4 * rows * model),
        )(
            plan,
            me,
            rots[DOWN_PERMUTE[s]],
            in_hbm(queries),
            in_hbm(less),
            in_hbm(rest),
            in_hbm(norm_gain.reshape(1, width)),
            in_hbm(out_proj.reshape(steps, step * HS, model)),
            *map(in_vmem, given),
        )

    def shared(pieces, permute):
        if group == 1:
            return pieces
        if not permute:
            return lax.all_to_all(pieces, "ctx", 0, 0, tiled=True, axis_index_groups=groups)
        outs = [pieces[:1]]
        for d in range(1, group):
            outs.append(lax.ppermute(pieces[d : d + 1], "ctx", [(i, i ^ d) for i in range(ctx)]))
        return outs

    mapped = [maps_of(s) for s in range(seqs)]
    gathered = [shared(maps, UP_PERMUTE[s]) for s, (maps, _) in enumerate(mapped)]
    reads = [reads_of(s, errors) for s, (_, errors) in enumerate(mapped)]
    gathered[0], reads = lax.optimization_barrier((gathered[0], reads))
    outs = []
    for s in range(seqs):
        moved = None
        for _ in range(ctx // group - 1):
            ending = chain(s, gathered[s], moved, False)
            moved = lax.ppermute(ending, "ctx", onward)
        leaving = chain(s, gathered[s], moved, True)
        entering = shared(leaving, DOWN_PERMUTE[s])
        products = final_of(s, reads[s], entering)
        total = products[0]
        for d in range(1, parts):
            other = lax.ppermute(products[d], "head", [(i, i ^ d) for i in range(parts)])
            total = total + other
        outs.append(total)
    return jnp.stack(outs, axis=1).astype(BF16)


def solution(mesh):
    return jax.shard_map(
        per_device,
        mesh=mesh,
        in_specs=(
            P(None, "ctx", "head"),
            P(None, "ctx", "head"),
            P(None, "ctx", "head"),
            P(None, "head", "ctx"),
            P("head"),
            P("head", None, None),
            P("head"),
            P("head", None),
            P(),
        ),
        out_specs=P(("ctx", "head"), None, None),
        check_vma=False,
    )
```

```python
import functools

import jax
import jax.numpy as jnp
from jax import lax
from jax.experimental import pallas as pl
from jax.experimental.pallas import tpu as pltpu
from jax.sharding import PartitionSpec as P


HS = 128
MB = 64
EPS = 1e-06
STEP = 8
WIDE = 512
SMALL = 14
LARGE = 30
UP_PERMUTE = (False, True)
DOWN_PERMUTE = (False, False)
F32 = jnp.float32
BF16 = jnp.bfloat16


def mm(a, b, dims=((1,), (0,))):
    return lax.dot_general(a, b, (dims, ((), ())), preferred_element_type=F32)


ROWS_BY_ROWS = ((1,), (1,))


def iotas(rows, cols):
    return tuple(lax.broadcasted_iota(jnp.int32, (rows, cols), axis) for axis in (0, 1))


def eta_rows(gate_ref, rate_ref, heads_step, sign):
    first = pl.program_id(0) * heads_step
    return [gate_ref[0, pl.ds(first + h, 1), :] * (sign * rate_ref[first + h]) for h in range(heads_step)]


def maps_kernel(heads_step, per, plan_ref, rot_ref, k_ref, v_ref, gate_ref, rate_ref, map_ref, t_ref):
    rows = k_ref.shape[1]
    pair = 2 * MB
    each = range(heads_step)
    etas = eta_rows(gate_ref, rate_ref, heads_step, 1.0)
    to, of = iotas(MB, pair)
    left, diag = of < MB, of == to + MB
    eye = jnp.where(jnp.equal(*iotas(pair, pair)), 1.0, 0.0).astype(BF16)
    ks = [k_ref[0, :, h * HS : (h + 1) * HS] for h in each]
    for h in each:
        t_ref[h] = jnp.concatenate([ks[h], -v_ref[0, :, h * HS : (h + 1) * HS]], axis=1)
    for begin in range(0, rows, pair):
        end, late = begin + pair, begin + MB
        if begin:
            reach = [-mm(ks[h][begin:end], ks[h][:begin], ROWS_BY_ROWS) * etas[h][:, :begin] for h in each]
            reach = [jnp.concatenate([r.astype(BF16), eye], axis=1) for r in reach]
            for h in each:
                t_ref[h, begin:end] = mm(reach[h], t_ref[h, :end]).astype(BF16)
        near = [-mm(ks[h][late:end], ks[h][begin:end], ROWS_BY_ROWS) * etas[h][:, begin:end] for h in each]
        near = [jnp.where(left, n, jnp.where(diag, 1.0, 0.0)).astype(BF16) for n in near]
        for h in each:
            t_ref[h, late:end] = mm(near[h], t_ref[h, begin:end]).astype(BF16)
    weighted = [(jnp.transpose(ks[h].astype(F32)) * etas[h]).astype(BF16) for h in each]
    for h in each:
        total = mm(weighted[h], t_ref[h])
        place = lax.rem(rot_ref[0], heads_step // per) ^ (h // per)
        map_ref[place, h % per, 0] = total[:, :HS]
        map_ref[place, h % per, 1] = total[:, HS:]


def reads_kernel(heads_step, plan_ref, q_ref, k_ref, gate_ref, rate_ref, t_ref, less_ref, rest_ref):
    rows = q_ref.shape[1]
    pair = 2 * MB
    each = range(heads_step)
    etas = eta_rows(gate_ref, rate_ref, heads_step, -1.0)
    lower = jnp.greater_equal(*iotas(pair, pair))
    for begin in range(0, rows, pair):
        end = begin + pair
        scores = []
        for h in each:
            cols = slice(h * HS, (h + 1) * HS)
            score = mm(q_ref[0, begin:end, cols], k_ref[0, :end, cols], ROWS_BY_ROWS) * etas[h][:, :end]
            parts = [score[:, :begin]] if begin else []
            parts.append(jnp.where(lower, score[:, begin:], 0.0))
            scores.append(jnp.concatenate(parts, axis=1).astype(BF16))
        for h in each:
            cols = slice(h * HS, (h + 1) * HS)
            taken = mm(scores[h], t_ref[h, :end])
            less_ref[begin:end, cols] = taken[:, :HS].astype(BF16)
            rest_ref[begin:end, cols] = taken[:, HS:].astype(BF16)


def advance(state, both):
    return state - mm(both[0].astype(BF16), state.astype(BF16)) - both[1]


def chain_kernel(group, hops, all_out, one, streamed, info_ref, start_ref, *refs):
    moved_ref, refs = (refs[0], refs[1:]) if hops else (None, refs)
    count = 1 if one else group
    maps, out_ref, held = refs[:count], refs[count], refs[count + 1 :]
    copies = []
    if streamed:
        far_ref, out_ref, sems = out_ref, held[-2], held[-1]
        copies = [pltpu.make_async_copy(out_ref.at[m], far_ref.at[m], sems.at[m]) for m in range(group)]
    if one:
        source = maps[0]
    else:
        source = held[0]
        for d in range(group):
            source[d ^ info_ref[0]] = maps[d][0]
    per = source.shape[1]
    states = [start_ref[u] for u in range(per)]
    if hops:
        states = [jnp.where(info_ref[1] == 0, states[u], moved_ref[u]) for u in range(per)]
    for m in range(group):
        for u in range(per):
            if all_out:
                out_ref[m if streamed else m ^ info_ref[2], u] = states[u]
            if not all_out or m < group - 1:
                states[u] = advance(states[u], source[m, u])
        if streamed:
            copies[m].start()
    for copy in copies:
        copy.wait()
    if not all_out:
        for u in range(per):
            out_ref[u] = states[u]


def final_kernel(steps, parts, group, plan_ref, me_ref, rot_ref, q_ref, less_ref, rest_ref, gain_ref, proj_ref, *refs):
    states, outs, (held, normed, proj, sems) = refs[:group], refs[group:-4], refs[-4:]
    piece = normed.shape[1] // parts
    i = pl.program_id(0)
    per = held.shape[1]

    wide = proj.shape[3]

    def chunk(c):
        part = proj_ref.at[:, :, pl.ds(pl.multiple_of(c * wide, wide), wide)]
        return pltpu.make_async_copy(part, proj.at[c], sems.at[c])

    @pl.when(i == 0)
    def _():
        for c in range(proj.shape[0]):
            chunk(c).start()
        for d in range(group):
            held[d ^ rot_ref[0]] = states[d][0]

    @pl.when(i < steps)
    def _():
        heads_step = normed.shape[2] // HS
        zs = []
        for h in range(heads_step):
            cols = slice(h * HS, (h + 1) * HS)
            state = held[i * (heads_step // per) + h // per, h % per]
            main = state.astype(BF16)
            small = (state - main.astype(F32)).astype(BF16)
            q = q_ref[0, :, cols]
            z = mm(jnp.concatenate([q, less_ref[:, cols]], axis=1), jnp.concatenate([main, main], axis=0))
            zs.append(z + mm(q, small) + rest_ref[:, cols].astype(F32))
        for h in range(heads_step):
            cols = slice(h * HS, (h + 1) * HS)
            scale = lax.rsqrt(jnp.mean(zs[h] * zs[h], axis=-1, keepdims=True) + EPS)
            out = (zs[h] * scale * gain_ref[:, cols]).astype(BF16)
            for p in range(parts):
                begin = pl.multiple_of((me_ref[0] ^ p) * piece, piece)
                normed[i, pl.ds(begin, piece), cols] = out[p * piece : (p + 1) * piece]

    @pl.when(i >= steps)
    def _():
        chunk(i - steps).wait()
        product = sum(mm(normed[n], proj[i - steps, n]) for n in range(steps))
        for d in range(parts):
            outs[d][...] = product[d * piece : (d + 1) * piece]


def sum_kernel(parts, *refs):
    seqs = len(refs[:-1]) // parts
    sums = [sum(ref[...] for ref in refs[s * parts : (s + 1) * parts]) for s in range(seqs)]
    rows = jnp.concatenate(sums, axis=0).astype(BF16)
    count, each = rows.shape[0], sums[0].shape[0]
    to, of = iotas(count, count)
    pick = jnp.where(lax.rem(to, seqs) * each + lax.div(to, seqs) == of, 1.0, 0.0).astype(BF16)
    refs[-1][...] = mm(pick, rows).astype(BF16).reshape(each, seqs, rows.shape[1])


def in_hbm(x):
    return pltpu.with_memory_space_constraint(x, pltpu.HBM)


def in_vmem(x):
    return pltpu.with_memory_space_constraint(x, pltpu.VMEM)


def limit(mib):
    return pltpu.CompilerParams(vmem_limit_bytes=mib * 2**20)


def cost(flops, nbytes):
    return pl.CostEstimate(flops=int(flops), bytes_accessed=int(nbytes), transcendentals=0)


def per_device(queries, keys, values, token_gate, head_rate, init_state, norm_gain, out_proj, plan):
    seqs, rows, width = queries.shape
    heads = init_state.shape[0]
    model = out_proj.shape[1]
    ctx, parts = lax.axis_size("ctx"), lax.axis_size("head")
    plan, head_rate = in_hbm(plan), in_hbm(head_rate)
    group = 1
    while group < 8 and heads % (2 * group) == 0 and ctx % (2 * group) == 0:
        group *= 2
    per = heads // group
    groups = [list(range(g, g + group)) for g in range(0, ctx, group)]
    onward = [(i, i + group) for i in range(ctx - group)]
    position = lax.axis_index("ctx").astype(jnp.int32)
    place, block = lax.rem(position, group), lax.div(position, group)
    rots = {True: place.reshape(1), False: jnp.zeros((1,), jnp.int32)}
    me = lax.axis_index("head").astype(jnp.int32).reshape(1)
    step = STEP if heads % STEP == 0 else heads
    smem = pl.BlockSpec(memory_space=pltpu.SMEM)

    def seq_block(s):
        return pl.BlockSpec((1, rows, step * HS), lambda i, plan_ref: (plan_ref[s], 0, i))

    def gate_block(s):
        return pl.BlockSpec((1, heads, rows), lambda i, plan_ref: (plan_ref[s], 0, 0))

    t_block = pl.BlockSpec((step, rows, 2 * HS), lambda i, plan_ref: (i, 0, 0))
    col_block = pl.BlockSpec((rows, step * HS), lambda i, plan_ref: (0, i))

    def maps_of(s):
        part = step // per
        grid_spec = pltpu.PrefetchScalarGridSpec(
            num_scalar_prefetch=2,
            grid=(heads // step,),
            in_specs=[
                pl.BlockSpec((1, rows, step * HS), lambda i, plan_ref, rot_ref: (plan_ref[s], 0, i)),
                pl.BlockSpec((1, rows, step * HS), lambda i, plan_ref, rot_ref: (plan_ref[s], 0, i)),
                pl.BlockSpec((1, heads, rows), lambda i, plan_ref, rot_ref: (plan_ref[s], 0, 0)),
                smem,
            ],
            out_specs=[
                pl.BlockSpec(
                    (part, per, 2, HS, HS),
                    lambda i, plan_ref, rot_ref: (lax.div(rot_ref[0], part) ^ i, 0, 0, 0, 0),
                ),
                pl.BlockSpec((step, rows, 2 * HS), lambda i, plan_ref, rot_ref: (i, 0, 0)),
            ],
        )
        return pl.pallas_call(
            functools.partial(maps_kernel, step, per),
            grid_spec=grid_spec,
            out_shape=[
                (pltpu.VMEM if UP_PERMUTE[s] else pltpu.HBM)((group, per, 2, HS, HS), F32),
                pltpu.HBM((heads, rows, 2 * HS), BF16),
            ],
            cost_estimate=cost(heads * 6 * rows * 256 * 256, heads * rows * HS * 12),
            compiler_params=limit(SMALL),
        )(plan, rots[UP_PERMUTE[s]], in_hbm(keys), in_hbm(values), in_hbm(token_gate), head_rate)

    def reads_of(s, errors):
        return pl.pallas_call(
            functools.partial(reads_kernel, step),
            grid_spec=pltpu.PrefetchScalarGridSpec(
                num_scalar_prefetch=1,
                grid=(heads // step,),
                in_specs=[seq_block(s), seq_block(s), gate_block(s), smem, t_block],
                out_specs=[col_block, col_block],
            ),
            out_shape=[
                pltpu.HBM((rows, width), BF16),
                pltpu.HBM((rows, width), BF16),
            ],
            cost_estimate=cost(heads * 8 * rows * 256 * 256, heads * rows * HS * 16),
            compiler_params=limit(SMALL),
        )(plan, in_hbm(queries), in_hbm(keys), in_hbm(token_gate), head_rate, in_hbm(errors))

    def one_of(parts_d, blocks):
        tail = (0,) * (len(blocks) - 1)
        if isinstance(parts_d, list):
            return parts_d, [pl.BlockSpec(blocks, lambda i, *_: (0,) + tail) for _ in parts_d]
        return [parts_d] * group, [pl.BlockSpec(blocks, lambda i, *_, d=d: (d,) + tail) for d in range(group)]

    start = lax.dynamic_slice_in_dim(init_state, place * per, per)

    def chain(s, gathered, moved, all_out):
        shape = (group, per, HS, HS) if all_out else (per, HS, HS)
        info = jnp.concatenate([rots[UP_PERMUTE[s]], block.reshape(1), rots[DOWN_PERMUTE[s]]])
        one = not isinstance(gathered, list)
        hops = moved is not None
        given = ([start, moved] if hops else [start]) + ([gathered] if one else gathered)
        vmem = pl.BlockSpec(memory_space=pltpu.VMEM)
        streamed = all_out and not DOWN_PERMUTE[s]
        scratch = [] if one else [pltpu.VMEM((group, per, 2, HS, HS), F32)]
        if streamed:
            scratch += [pltpu.VMEM(shape, F32), pltpu.SemaphoreType.DMA((group,))]
        return pl.pallas_call(
            functools.partial(chain_kernel, group, hops, all_out, one, streamed),
            in_specs=[smem] + [vmem] * len(given),
            out_specs=pl.BlockSpec(memory_space=pltpu.HBM) if streamed else vmem,
            scratch_shapes=scratch,
            out_shape=pltpu.HBM(shape, F32) if streamed else jax.ShapeDtypeStruct(shape, F32),
            compiler_params=limit(SMALL),
            cost_estimate=cost(group * per * 6 * HS**3, group * per * HS * HS * 12),
        )(info, *map(in_vmem, given))

    wide = WIDE if model % WIDE == 0 else model
    steps = heads // step

    def final_of(s, reads, entering):
        less, rest = reads
        piece = rows // parts
        early = lambda i: jnp.minimum(i, steps - 1)
        late = lambda i: jnp.maximum(i - steps, 0)
        by_cols = pl.BlockSpec((rows, step * HS), lambda i, *_: (0, early(i)))
        given, state_specs = one_of(entering, (1, per, HS, HS))
        return pl.pallas_call(
            functools.partial(final_kernel, steps, parts, group),
            grid_spec=pltpu.PrefetchScalarGridSpec(
                num_scalar_prefetch=3,
                grid=(steps + model // wide,),
                in_specs=[
                    pl.BlockSpec((1, rows, step * HS), lambda i, plan_ref, *_: (plan_ref[s], 0, early(i))),
                    by_cols,
                    by_cols,
                    pl.BlockSpec((1, step * HS), lambda i, *_: (0, early(i))),
                    pl.BlockSpec(memory_space=pltpu.HBM),
                ]
                + state_specs,
                out_specs=[pl.BlockSpec((piece, wide), lambda i, *_: (0, late(i)))] * parts,
                scratch_shapes=[
                    pltpu.VMEM((group, per, HS, HS), F32),
                    pltpu.VMEM((steps, rows, step * HS), BF16),
                    pltpu.VMEM((model // wide, steps, step * HS, wide), BF16),
                    pltpu.SemaphoreType.DMA((model // wide,)),
                ],
            ),
            compiler_params=limit(LARGE),
            out_shape=[jax.ShapeDtypeStruct((piece, model), F32)] * parts,
            cost_estimate=cost(2 * rows * width * model, 2 * width * model + 4 * rows * model),
        )(
            plan,
            me,
            rots[DOWN_PERMUTE[s]],
            in_hbm(queries),
            in_hbm(less),
            in_hbm(rest),
            in_hbm(norm_gain.reshape(1, width)),
            in_hbm(out_proj.reshape(steps, step * HS, model)),
            *map(in_vmem, given),
        )

    def shared(pieces, permute):
        if group == 1:
            return pieces
        if not permute:
            return lax.all_to_all(pieces, "ctx", 0, 0, tiled=True, axis_index_groups=groups)
        outs = [pieces[:1]]
        for d in range(1, group):
            outs.append(lax.ppermute(pieces[d : d + 1], "ctx", [(i, i ^ d) for i in range(ctx)]))
        return outs

    mapped = [maps_of(s) for s in range(seqs)]
    gathered = [shared(maps, UP_PERMUTE[s]) for s, (maps, _) in enumerate(mapped)]
    reads = [reads_of(s, errors) for s, (_, errors) in enumerate(mapped)]
    gathered[0], reads = lax.optimization_barrier((gathered[0], reads))
    outs = []
    for s in range(seqs):
        moved = None
        for _ in range(ctx // group - 1):
            ending = chain(s, gathered[s], moved, False)
            moved = lax.ppermute(ending, "ctx", onward)
        leaving = chain(s, gathered[s], moved, True)
        entering = shared(leaving, DOWN_PERMUTE[s])
        products = final_of(s, reads[s], entering)
        outs.append(products[0])
        for d in range(1, parts):
            outs.append(lax.ppermute(products[d], "head", [(i, i ^ d) for i in range(parts)]))
    piece = rows // parts
    wider = 2048 if model % 2048 == 0 else model
    return pl.pallas_call(
        functools.partial(sum_kernel, parts),
        grid=(model // wider,),
        in_specs=[pl.BlockSpec((piece, wider), lambda i: (0, i))] * len(outs),
        out_specs=pl.BlockSpec((piece, seqs, wider), lambda i: (0, 0, i)),
        out_shape=jax.ShapeDtypeStruct((piece, seqs, model), BF16),
        compiler_params=limit(2 * SMALL),
        cost_estimate=cost(2 * (piece * seqs) ** 2 * model, 4 * len(outs) * piece * model),
        name="sums",
    )(*outs)


def solution(mesh):
    return jax.shard_map(
        per_device,
        mesh=mesh,
        in_specs=(
            P(None, "ctx", "head"),
            P(None, "ctx", "head"),
            P(None, "ctx", "head"),
            P(None, "head", "ctx"),
            P("head"),
            P("head", None, None),
            P("head"),
            P("head", None),
            P(),
        ),
        out_specs=P(("ctx", "head"), None, None),
        check_vma=False,
    )
```

```python
import functools

import jax
import jax.numpy as jnp
from jax import lax
from jax.experimental import pallas as pl
from jax.experimental.pallas import tpu as pltpu
from jax.sharding import PartitionSpec as P


HS = 128
MB = 64
EPS = 1e-06
STEP = 8
WIDE = 1024
SMALL = 14
LARGE = 30
UP_PERMUTE = (True, False)
DOWN_PERMUTE = (False, False)
F32 = jnp.float32
BF16 = jnp.bfloat16


def mm(a, b, dims=((1,), (0,))):
    return lax.dot_general(a, b, (dims, ((), ())), preferred_element_type=F32)


ROWS_BY_ROWS = ((1,), (1,))


def iotas(rows, cols):
    return tuple(lax.broadcasted_iota(jnp.int32, (rows, cols), axis) for axis in (0, 1))


def eta_rows(gate_ref, rate_ref, heads_step, sign):
    first = pl.program_id(0) * heads_step
    return [gate_ref[0, pl.ds(first + h, 1), :] * (sign * rate_ref[first + h]) for h in range(heads_step)]


def maps_kernel(heads_step, per, plan_ref, rot_ref, k_ref, v_ref, gate_ref, rate_ref, map_ref, t_ref):
    rows = k_ref.shape[1]
    pair = 2 * MB
    each = range(heads_step)
    etas = eta_rows(gate_ref, rate_ref, heads_step, 1.0)
    to, of = iotas(MB, pair)
    left, diag = of < MB, of == to + MB
    eye = jnp.where(jnp.equal(*iotas(pair, pair)), 1.0, 0.0).astype(BF16)
    ks = [k_ref[0, :, h * HS : (h + 1) * HS] for h in each]
    for h in each:
        t_ref[h] = jnp.concatenate([ks[h], -v_ref[0, :, h * HS : (h + 1) * HS]], axis=1)
    for begin in range(0, rows, pair):
        end, late = begin + pair, begin + MB
        if begin:
            reach = [-mm(ks[h][begin:end], ks[h][:begin], ROWS_BY_ROWS) * etas[h][:, :begin] for h in each]
            reach = [jnp.concatenate([r.astype(BF16), eye], axis=1) for r in reach]
            for h in each:
                t_ref[h, begin:end] = mm(reach[h], t_ref[h, :end]).astype(BF16)
        near = [-mm(ks[h][late:end], ks[h][begin:end], ROWS_BY_ROWS) * etas[h][:, begin:end] for h in each]
        near = [jnp.where(left, n, jnp.where(diag, 1.0, 0.0)).astype(BF16) for n in near]
        for h in each:
            t_ref[h, late:end] = mm(near[h], t_ref[h, begin:end]).astype(BF16)
    weighted = [(jnp.transpose(ks[h].astype(F32)) * etas[h]).astype(BF16) for h in each]
    for h in each:
        total = mm(weighted[h], t_ref[h])
        place = lax.rem(rot_ref[0], heads_step // per) ^ (h // per)
        map_ref[place, h % per, 0] = total[:, :HS]
        map_ref[place, h % per, 1] = total[:, HS:]


def reads_kernel(heads_step, plan_ref, q_ref, k_ref, gate_ref, rate_ref, t_ref, less_ref, rest_ref):
    rows = q_ref.shape[1]
    pair = 2 * MB
    each = range(heads_step)
    etas = eta_rows(gate_ref, rate_ref, heads_step, -1.0)
    lower = jnp.greater_equal(*iotas(pair, pair))
    for begin in range(0, rows, pair):
        end = begin + pair
        scores = []
        for h in each:
            cols = slice(h * HS, (h + 1) * HS)
            score = mm(q_ref[0, begin:end, cols], k_ref[0, :end, cols], ROWS_BY_ROWS) * etas[h][:, :end]
            parts = [score[:, :begin]] if begin else []
            parts.append(jnp.where(lower, score[:, begin:], 0.0))
            scores.append(jnp.concatenate(parts, axis=1).astype(BF16))
        for h in each:
            cols = slice(h * HS, (h + 1) * HS)
            taken = mm(scores[h], t_ref[h, :end])
            less_ref[begin:end, cols] = taken[:, :HS].astype(BF16)
            rest_ref[begin:end, cols] = taken[:, HS:].astype(BF16)


def advance(state, both):
    return state - mm(both[0].astype(BF16), state.astype(BF16)) - both[1]


def chain_kernel(group, hops, all_out, kind, streamed, info_ref, start_ref, *refs):
    moved_ref, refs = (refs[0], refs[1:]) if hops else (None, refs)
    count = group if kind == "pieces" else 1
    maps, out_ref, held = refs[:count], refs[count], list(refs[count + 1 :])
    arrivals, copies = [], []
    source = maps[0]
    if kind == "pieces":
        source = held.pop(0)
        for d in range(group):
            source[d ^ info_ref[0]] = maps[d][0]
    elif kind == "far":
        source, sems = held.pop(0), held.pop(0)
        arrivals = [pltpu.make_async_copy(maps[0].at[m], source.at[m], sems.at[m]) for m in range(group)]
        for arrival in arrivals:
            arrival.start()
    if streamed:
        far_ref, out_ref, sems = out_ref, held[0], held[1]
        copies = [pltpu.make_async_copy(out_ref.at[m], far_ref.at[m], sems.at[m]) for m in range(group)]
    per = source.shape[1]
    states = [start_ref[u] for u in range(per)]
    if hops:
        states = [jnp.where(info_ref[1] == 0, states[u], moved_ref[u]) for u in range(per)]
    for m in range(group):
        if arrivals:
            arrivals[m].wait()
        for u in range(per):
            if all_out:
                out_ref[m if streamed else m ^ info_ref[2], u] = states[u]
            if not all_out or m < group - 1:
                states[u] = advance(states[u], source[m, u])
        if streamed:
            copies[m].start()
    for copy in copies:
        copy.wait()
    if not all_out:
        for u in range(per):
            out_ref[u] = states[u]


def final_kernel(steps, parts, group, plan_ref, me_ref, rot_ref, q_ref, less_ref, rest_ref, gain_ref, proj_ref, *refs):
    states, outs, (held, normed, proj, sems) = refs[:group], refs[group:-4], refs[-4:]
    piece = normed.shape[1] // parts
    i = pl.program_id(0)
    per = held.shape[1]

    wide = proj.shape[3]

    def chunk(c):
        part = proj_ref.at[:, :, pl.ds(pl.multiple_of(c * wide, wide), wide)]
        return pltpu.make_async_copy(part, proj.at[c], sems.at[c])

    @pl.when(i == 0)
    def _():
        for c in range(proj.shape[0]):
            chunk(c).start()
        for d in range(group):
            held[d ^ rot_ref[0]] = states[d][0]

    @pl.when(i < steps)
    def _():
        heads_step = normed.shape[2] // HS
        none = jnp.zeros((HS, HS), BF16)
        zs = []
        for h in range(heads_step):
            cols = slice(h * HS, (h + 1) * HS)
            state = held[i * (heads_step // per) + h // per, h % per]
            main = state.astype(BF16)
            small = (state - main.astype(F32)).astype(BF16)
            left = jnp.concatenate([q_ref[0, :, cols], less_ref[:, cols]], axis=1)
            top, bottom = jnp.concatenate([main, small], axis=1), jnp.concatenate([main, none], axis=1)
            both = mm(left, jnp.concatenate([top, bottom], axis=0))
            zs.append(both[:, :HS] + both[:, HS:] + rest_ref[:, cols].astype(F32))
        for h in range(heads_step):
            cols = slice(h * HS, (h + 1) * HS)
            scale = lax.rsqrt(jnp.mean(zs[h] * zs[h], axis=-1, keepdims=True) + EPS)
            out = (zs[h] * scale * gain_ref[:, cols]).astype(BF16)
            for p in range(parts):
                begin = pl.multiple_of((me_ref[0] ^ p) * piece, piece)
                normed[i, pl.ds(begin, piece), cols] = out[p * piece : (p + 1) * piece]

    @pl.when(i >= steps)
    def _():
        chunk(i - steps).wait()
        product = sum(mm(normed[n], proj[i - steps, n]) for n in range(steps))
        for d in range(parts):
            outs[d][...] = product[d * piece : (d + 1) * piece]


def sum_kernel(parts, *refs):
    seqs = len(refs[:-1]) // parts
    sums = [sum(ref[...] for ref in refs[s * parts : (s + 1) * parts]) for s in range(seqs)]
    rows = jnp.concatenate(sums, axis=0).astype(BF16)
    count, each = rows.shape[0], sums[0].shape[0]
    to, of = iotas(count, count)
    pick = jnp.where(lax.rem(to, seqs) * each + lax.div(to, seqs) == of, 1.0, 0.0).astype(BF16)
    refs[-1][...] = mm(pick, rows).astype(BF16).reshape(each, seqs, rows.shape[1])


def in_hbm(x):
    return pltpu.with_memory_space_constraint(x, pltpu.HBM)


def in_vmem(x):
    return pltpu.with_memory_space_constraint(x, pltpu.VMEM)


def limit(mib):
    return pltpu.CompilerParams(vmem_limit_bytes=mib * 2**20)


def cost(flops, nbytes):
    return pl.CostEstimate(flops=int(flops), bytes_accessed=int(nbytes), transcendentals=0)


def per_device(queries, keys, values, token_gate, head_rate, init_state, norm_gain, out_proj, plan):
    seqs, rows, width = queries.shape
    heads = init_state.shape[0]
    model = out_proj.shape[1]
    ctx, parts = lax.axis_size("ctx"), lax.axis_size("head")
    plan, head_rate = in_hbm(plan), in_hbm(head_rate)
    group = 1
    while group < 8 and heads % (2 * group) == 0 and ctx % (2 * group) == 0:
        group *= 2
    per = heads // group
    groups = [list(range(g, g + group)) for g in range(0, ctx, group)]
    onward = [(i, i + group) for i in range(ctx - group)]
    position = lax.axis_index("ctx").astype(jnp.int32)
    place, block = lax.rem(position, group), lax.div(position, group)
    rots = {True: place.reshape(1), False: jnp.zeros((1,), jnp.int32)}
    me = lax.axis_index("head").astype(jnp.int32).reshape(1)
    step = STEP if heads % STEP == 0 else heads
    smem = pl.BlockSpec(memory_space=pltpu.SMEM)

    def seq_block(s):
        return pl.BlockSpec((1, rows, step * HS), lambda i, plan_ref: (plan_ref[s], 0, i))

    def gate_block(s):
        return pl.BlockSpec((1, heads, rows), lambda i, plan_ref: (plan_ref[s], 0, 0))

    t_block = pl.BlockSpec((step, rows, 2 * HS), lambda i, plan_ref: (i, 0, 0))
    col_block = pl.BlockSpec((rows, step * HS), lambda i, plan_ref: (0, i))

    def maps_of(s):
        part = step // per
        grid_spec = pltpu.PrefetchScalarGridSpec(
            num_scalar_prefetch=2,
            grid=(heads // step,),
            in_specs=[
                pl.BlockSpec((1, rows, step * HS), lambda i, plan_ref, rot_ref: (plan_ref[s], 0, i)),
                pl.BlockSpec((1, rows, step * HS), lambda i, plan_ref, rot_ref: (plan_ref[s], 0, i)),
                pl.BlockSpec((1, heads, rows), lambda i, plan_ref, rot_ref: (plan_ref[s], 0, 0)),
                smem,
            ],
            out_specs=[
                pl.BlockSpec(
                    (part, per, 2, HS, HS),
                    lambda i, plan_ref, rot_ref: (lax.div(rot_ref[0], part) ^ i, 0, 0, 0, 0),
                ),
                pl.BlockSpec((step, rows, 2 * HS), lambda i, plan_ref, rot_ref: (i, 0, 0)),
            ],
        )
        return pl.pallas_call(
            functools.partial(maps_kernel, step, per),
            grid_spec=grid_spec,
            out_shape=[
                (pltpu.VMEM if UP_PERMUTE[s] else pltpu.HBM)((group, per, 2, HS, HS), F32),
                pltpu.HBM((heads, rows, 2 * HS), BF16),
            ],
            cost_estimate=cost(heads * 6 * rows * 256 * 256, heads * rows * HS * 12),
            compiler_params=limit(SMALL),
        )(plan, rots[UP_PERMUTE[s]], in_hbm(keys), in_hbm(values), in_hbm(token_gate), head_rate)

    def reads_of(s, errors):
        return pl.pallas_call(
            functools.partial(reads_kernel, step),
            grid_spec=pltpu.PrefetchScalarGridSpec(
                num_scalar_prefetch=1,
                grid=(heads // step,),
                in_specs=[seq_block(s), seq_block(s), gate_block(s), smem, t_block],
                out_specs=[col_block, col_block],
            ),
            out_shape=[
                pltpu.HBM((rows, width), BF16),
                pltpu.HBM((rows, width), BF16),
            ],
            cost_estimate=cost(heads * 8 * rows * 256 * 256, heads * rows * HS * 16),
            compiler_params=limit(SMALL),
        )(plan, in_hbm(queries), in_hbm(keys), in_hbm(token_gate), head_rate, in_hbm(errors))

    def one_of(parts_d, blocks):
        tail = (0,) * (len(blocks) - 1)
        if isinstance(parts_d, list):
            return parts_d, [pl.BlockSpec(blocks, lambda i, *_: (0,) + tail) for _ in parts_d]
        return [parts_d] * group, [pl.BlockSpec(blocks, lambda i, *_, d=d: (d,) + tail) for d in range(group)]

    start = lax.dynamic_slice_in_dim(init_state, place * per, per)

    def chain(s, gathered, moved, all_out):
        shape = (group, per, HS, HS) if all_out else (per, HS, HS)
        info = jnp.concatenate([rots[UP_PERMUTE[s]], block.reshape(1), rots[DOWN_PERMUTE[s]]])
        kind = "pieces" if isinstance(gathered, list) else "far" if s else "near"
        hops = moved is not None
        given = [start, moved] if hops else [start]
        vmem, hbm = pl.BlockSpec(memory_space=pltpu.VMEM), pl.BlockSpec(memory_space=pltpu.HBM)
        given = [in_vmem(x) for x in given]
        specs = [smem] + [vmem] * len(given)
        pieces = gathered if kind == "pieces" else [gathered]
        given += [in_hbm(x) if kind == "far" else in_vmem(x) for x in pieces]
        specs += [hbm if kind == "far" else vmem] * len(pieces)
        streamed = all_out and not DOWN_PERMUTE[s]
        scratch = [] if kind == "near" else [pltpu.VMEM((group, per, 2, HS, HS), F32)]
        if kind == "far":
            scratch.append(pltpu.SemaphoreType.DMA((group,)))
        if streamed:
            scratch += [pltpu.VMEM(shape, F32), pltpu.SemaphoreType.DMA((group,))]
        return pl.pallas_call(
            functools.partial(chain_kernel, group, hops, all_out, kind, streamed),
            in_specs=specs,
            out_specs=hbm if streamed else vmem,
            scratch_shapes=scratch,
            out_shape=pltpu.HBM(shape, F32) if streamed else jax.ShapeDtypeStruct(shape, F32),
            compiler_params=limit(SMALL),
            cost_estimate=cost(group * per * 6 * HS**3, group * per * HS * HS * 12),
        )(info, *given)

    wide = WIDE if model % WIDE == 0 else model
    steps = heads // step

    def final_of(s, reads, entering):
        less, rest = reads
        piece = rows // parts
        early = lambda i: jnp.minimum(i, steps - 1)
        late = lambda i: jnp.maximum(i - steps, 0)
        by_cols = pl.BlockSpec((rows, step * HS), lambda i, *_: (0, early(i)))
        given, state_specs = one_of(entering, (1, per, HS, HS))
        return pl.pallas_call(
            functools.partial(final_kernel, steps, parts, group),
            grid_spec=pltpu.PrefetchScalarGridSpec(
                num_scalar_prefetch=3,
                grid=(steps + model // wide,),
                in_specs=[
                    pl.BlockSpec((1, rows, step * HS), lambda i, plan_ref, *_: (plan_ref[s], 0, early(i))),
                    by_cols,
                    by_cols,
                    pl.BlockSpec((1, step * HS), lambda i, *_: (0, early(i))),
                    pl.BlockSpec(memory_space=pltpu.HBM),
                ]
                + state_specs,
                out_specs=[pl.BlockSpec((piece, wide), lambda i, *_: (0, late(i)))] * parts,
                scratch_shapes=[
                    pltpu.VMEM((group, per, HS, HS), F32),
                    pltpu.VMEM((steps, rows, step * HS), BF16),
                    pltpu.VMEM((model // wide, steps, step * HS, wide), BF16),
                    pltpu.SemaphoreType.DMA((model // wide,)),
                ],
            ),
            compiler_params=limit(LARGE),
            out_shape=[(pltpu.HBM if s < seqs - 1 else pltpu.VMEM)((piece, model), F32)] * parts,
            cost_estimate=cost(2 * rows * width * model, 2 * width * model + 4 * rows * model),
        )(
            plan,
            me,
            rots[DOWN_PERMUTE[s]],
            in_hbm(queries),
            in_hbm(less),
            in_hbm(rest),
            in_hbm(norm_gain.reshape(1, width)),
            in_hbm(out_proj.reshape(steps, step * HS, model)),
            *map(in_vmem, given),
        )

    def shared(pieces, permute):
        if group == 1:
            return pieces
        if not permute:
            return lax.all_to_all(pieces, "ctx", 0, 0, tiled=True, axis_index_groups=groups)
        outs = [pieces[:1]]
        for d in range(1, group):
            outs.append(lax.ppermute(pieces[d : d + 1], "ctx", [(i, i ^ d) for i in range(ctx)]))
        return outs

    mapped = [maps_of(s) for s in range(seqs)]
    gathered = [shared(maps, UP_PERMUTE[s]) for s, (maps, _) in enumerate(mapped)]
    reads = [reads_of(s, errors) for s, (_, errors) in enumerate(mapped)]
    gathered[0], reads = lax.optimization_barrier((gathered[0], reads))
    outs = []
    for s in range(seqs):
        moved = None
        for _ in range(ctx // group - 1):
            ending = chain(s, gathered[s], moved, False)
            moved = lax.ppermute(ending, "ctx", onward)
        leaving = chain(s, gathered[s], moved, True)
        entering = shared(leaving, DOWN_PERMUTE[s])
        products = final_of(s, reads[s], entering)
        outs.append(products[0])
        for d in range(1, parts):
            outs.append(lax.ppermute(products[d], "head", [(i, i ^ d) for i in range(parts)]))
    piece = rows // parts
    wider = 2048 if model % 2048 == 0 else model
    return pl.pallas_call(
        functools.partial(sum_kernel, parts),
        grid=(model // wider,),
        in_specs=[pl.BlockSpec((piece, wider), lambda i: (0, i))] * len(outs),
        out_specs=pl.BlockSpec((piece, seqs, wider), lambda i: (0, 0, i)),
        out_shape=jax.ShapeDtypeStruct((piece, seqs, model), BF16),
        compiler_params=limit(2 * SMALL),
        cost_estimate=cost(2 * (piece * seqs) ** 2 * model, 4 * len(outs) * piece * model),
        name="sums",
    )(*outs)


def solution(mesh):
    return jax.shard_map(
        per_device,
        mesh=mesh,
        in_specs=(
            P(None, "ctx", "head"),
            P(None, "ctx", "head"),
            P(None, "ctx", "head"),
            P(None, "head", "ctx"),
            P("head"),
            P("head", None, None),
            P("head"),
            P("head", None),
            P(),
        ),
        out_specs=P(("ctx", "head"), None, None),
        check_vma=False,
    )
```

```python
import functools

import jax
import jax.numpy as jnp
from jax import lax
from jax.experimental import pallas as pl
from jax.experimental.pallas import tpu as pltpu
from jax.sharding import PartitionSpec as P


HS = 128
MB = 64
EPS = 1e-06
STEP = 8
WIDE = 1024
SMALL = 14
LARGE = 30
UP_PERMUTE = (True, False)
DOWN_PERMUTE = (False, False)
F32 = jnp.float32
BF16 = jnp.bfloat16


def mm(a, b, dims=((1,), (0,))):
    return lax.dot_general(a, b, (dims, ((), ())), preferred_element_type=F32)


ROWS_BY_ROWS = ((1,), (1,))


def iotas(rows, cols):
    return tuple(lax.broadcasted_iota(jnp.int32, (rows, cols), axis) for axis in (0, 1))


def eta_rows(gate_ref, rate_ref, heads_step, sign):
    first = pl.program_id(0) * heads_step
    return [gate_ref[0, pl.ds(first + h, 1), :] * (sign * rate_ref[first + h]) for h in range(heads_step)]


def maps_kernel(heads_step, per, plan_ref, rot_ref, k_ref, v_ref, gate_ref, rate_ref, map_ref, t_ref):
    rows = k_ref.shape[1]
    pair = 2 * MB
    each = range(heads_step)
    etas = eta_rows(gate_ref, rate_ref, heads_step, 1.0)
    to, of = iotas(MB, pair)
    left, diag = of < MB, of == to + MB
    eye = jnp.where(jnp.equal(*iotas(pair, pair)), 1.0, 0.0).astype(BF16)
    ks = [k_ref[0, :, h * HS : (h + 1) * HS] for h in each]
    for h in each:
        t_ref[h] = jnp.concatenate([ks[h], -v_ref[0, :, h * HS : (h + 1) * HS]], axis=1)
    for begin in range(0, rows, pair):
        end, late = begin + pair, begin + MB
        if begin:
            reach = [-mm(ks[h][begin:end], ks[h][:begin], ROWS_BY_ROWS) * etas[h][:, :begin] for h in each]
            reach = [jnp.concatenate([r.astype(BF16), eye], axis=1) for r in reach]
            for h in each:
                t_ref[h, begin:end] = mm(reach[h], t_ref[h, :end]).astype(BF16)
        near = [-mm(ks[h][late:end], ks[h][begin:end], ROWS_BY_ROWS) * etas[h][:, begin:end] for h in each]
        near = [jnp.where(left, n, jnp.where(diag, 1.0, 0.0)).astype(BF16) for n in near]
        for h in each:
            t_ref[h, late:end] = mm(near[h], t_ref[h, begin:end]).astype(BF16)
    weighted = [(jnp.transpose(ks[h].astype(F32)) * etas[h]).astype(BF16) for h in each]
    for h in each:
        total = mm(weighted[h], t_ref[h])
        place = lax.rem(rot_ref[0], heads_step // per) ^ (h // per)
        map_ref[place, h % per, 0] = total[:, :HS]
        map_ref[place, h % per, 1] = total[:, HS:]


def reads_kernel(heads_step, plan_ref, q_ref, k_ref, gate_ref, rate_ref, t_ref, less_ref, rest_ref):
    rows = q_ref.shape[1]
    pair = 2 * MB
    each = range(heads_step)
    etas = eta_rows(gate_ref, rate_ref, heads_step, -1.0)
    lower = jnp.greater_equal(*iotas(pair, pair))
    for begin in range(0, rows, pair):
        end = begin + pair
        scores = []
        for h in each:
            cols = slice(h * HS, (h + 1) * HS)
            score = mm(q_ref[0, begin:end, cols], k_ref[0, :end, cols], ROWS_BY_ROWS) * etas[h][:, :end]
            parts = [score[:, :begin]] if begin else []
            parts.append(jnp.where(lower, score[:, begin:], 0.0))
            scores.append(jnp.concatenate(parts, axis=1).astype(BF16))
        for h in each:
            cols = slice(h * HS, (h + 1) * HS)
            taken = mm(scores[h], t_ref[h, :end])
            less_ref[begin:end, cols] = taken[:, :HS].astype(BF16)
            rest_ref[begin:end, cols] = taken[:, HS:].astype(BF16)


def advance(state, both):
    return state - mm(both[0].astype(BF16), state.astype(BF16)) - both[1]


def chain_kernel(group, hops, all_out, kind, streamed, info_ref, start_ref, *refs):
    moved_ref, refs = (refs[0], refs[1:]) if hops else (None, refs)
    count = group if kind == "pieces" else 1
    maps, out_ref, held = refs[:count], refs[count], list(refs[count + 1 :])
    arrivals, copies = [], []
    source = maps[0]
    if kind == "pieces":
        source = held.pop(0)
        for d in range(group):
            source[d ^ info_ref[0]] = maps[d][0]
    elif kind == "far":
        source, sems = held.pop(0), held.pop(0)
        arrivals = [pltpu.make_async_copy(maps[0].at[m], source.at[m], sems.at[m]) for m in range(group)]
        for arrival in arrivals:
            arrival.start()
    if streamed:
        far_ref, out_ref, sems = out_ref, held[0], held[1]
        copies = [pltpu.make_async_copy(out_ref.at[m], far_ref.at[m], sems.at[m]) for m in range(group)]
    per = source.shape[1]
    states = [start_ref[u] for u in range(per)]
    if hops:
        states = [jnp.where(info_ref[1] == 0, states[u], moved_ref[u]) for u in range(per)]
    for m in range(group):
        if arrivals:
            arrivals[m].wait()
        for u in range(per):
            if all_out:
                out_ref[m if streamed else m ^ info_ref[2], u] = states[u]
            if not all_out or m < group - 1:
                states[u] = advance(states[u], source[m, u])
        if streamed:
            copies[m].start()
    for copy in copies:
        copy.wait()
    if not all_out:
        for u in range(per):
            out_ref[u] = states[u]


def final_kernel(steps, parts, group, plan_ref, me_ref, rot_ref, q_ref, less_ref, rest_ref, gain_ref, proj_ref, *refs):
    states, outs, (held, normed, proj, sems) = refs[:group], refs[group:-4], refs[-4:]
    piece = normed.shape[1] // parts
    i = pl.program_id(0)
    per = held.shape[1]

    wide = proj.shape[3]

    def chunk(c):
        part = proj_ref.at[:, :, pl.ds(pl.multiple_of(c * wide, wide), wide)]
        return pltpu.make_async_copy(part, proj.at[c], sems.at[c])

    @pl.when(i == 0)
    def _():
        for c in range(proj.shape[0]):
            chunk(c).start()
        for d in range(group):
            held[d ^ rot_ref[0]] = states[d][0]

    @pl.when(i < steps)
    def _():
        heads_step = normed.shape[2] // HS
        none = jnp.zeros((HS, HS), BF16)
        zs = []
        for h in range(heads_step):
            cols = slice(h * HS, (h + 1) * HS)
            state = held[i * (heads_step // per) + h // per, h % per]
            main = state.astype(BF16)
            small = (state - main.astype(F32)).astype(BF16)
            left = jnp.concatenate([q_ref[0, :, cols], less_ref[:, cols]], axis=1)
            top, bottom = jnp.concatenate([main, small], axis=1), jnp.concatenate([main, none], axis=1)
            both = mm(left, jnp.concatenate([top, bottom], axis=0))
            zs.append(both[:, :HS] + both[:, HS:] + rest_ref[:, cols].astype(F32))
        for h in range(heads_step):
            cols = slice(h * HS, (h + 1) * HS)
            scale = lax.rsqrt(jnp.mean(zs[h] * zs[h], axis=-1, keepdims=True) + EPS)
            out = (zs[h] * scale * gain_ref[:, cols]).astype(BF16)
            for p in range(parts):
                begin = pl.multiple_of((me_ref[0] ^ p) * piece, piece)
                normed[i, pl.ds(begin, piece), cols] = out[p * piece : (p + 1) * piece]

    @pl.when(i >= steps)
    def _():
        chunk(i - steps).wait()
        product = sum(mm(normed[n], proj[i - steps, n]) for n in range(steps))
        for d in range(parts):
            outs[d][...] = product[d * piece : (d + 1) * piece]


def sum_kernel(parts, *refs):
    seqs = len(refs[:-1]) // parts
    sums = [sum(ref[...] for ref in refs[s * parts : (s + 1) * parts]) for s in range(seqs)]
    rows = jnp.concatenate(sums, axis=0).astype(BF16)
    count, each = rows.shape[0], sums[0].shape[0]
    to, of = iotas(count, count)
    pick = jnp.where(lax.rem(to, seqs) * each + lax.div(to, seqs) == of, 1.0, 0.0).astype(BF16)
    refs[-1][...] = mm(pick, rows).astype(BF16).reshape(each, seqs, rows.shape[1])


def in_hbm(x):
    return pltpu.with_memory_space_constraint(x, pltpu.HBM)


def in_vmem(x):
    return pltpu.with_memory_space_constraint(x, pltpu.VMEM)


def limit(mib):
    return pltpu.CompilerParams(vmem_limit_bytes=mib * 2**20)


def cost(flops, nbytes):
    return pl.CostEstimate(flops=int(flops), bytes_accessed=int(nbytes), transcendentals=0)


def per_device(queries, keys, values, token_gate, head_rate, init_state, norm_gain, out_proj, plan):
    seqs, rows, width = queries.shape
    heads = init_state.shape[0]
    model = out_proj.shape[1]
    ctx, parts = lax.axis_size("ctx"), lax.axis_size("head")
    plan, head_rate = in_hbm(plan), in_hbm(head_rate)
    group = 1
    while group < 8 and heads % (2 * group) == 0 and ctx % (2 * group) == 0:
        group *= 2
    per = heads // group
    groups = [list(range(g, g + group)) for g in range(0, ctx, group)]
    onward = [(i, i + group) for i in range(ctx - group)]
    position = lax.axis_index("ctx").astype(jnp.int32)
    place, block = lax.rem(position, group), lax.div(position, group)
    rots = {True: place.reshape(1), False: jnp.zeros((1,), jnp.int32)}
    me = lax.axis_index("head").astype(jnp.int32).reshape(1)
    step = STEP if heads % STEP == 0 else heads
    smem = pl.BlockSpec(memory_space=pltpu.SMEM)

    def seq_block(s):
        return pl.BlockSpec((1, rows, step * HS), lambda i, plan_ref: (plan_ref[s], 0, i))

    def gate_block(s):
        return pl.BlockSpec((1, heads, rows), lambda i, plan_ref: (plan_ref[s], 0, 0))

    t_block = pl.BlockSpec((step, rows, 2 * HS), lambda i, plan_ref: (i, 0, 0))
    col_block = pl.BlockSpec((rows, step * HS), lambda i, plan_ref: (0, i))

    def maps_of(s):
        part = step // per
        grid_spec = pltpu.PrefetchScalarGridSpec(
            num_scalar_prefetch=2,
            grid=(heads // step,),
            in_specs=[
                pl.BlockSpec((1, rows, step * HS), lambda i, plan_ref, rot_ref: (plan_ref[s], 0, i)),
                pl.BlockSpec((1, rows, step * HS), lambda i, plan_ref, rot_ref: (plan_ref[s], 0, i)),
                pl.BlockSpec((1, heads, rows), lambda i, plan_ref, rot_ref: (plan_ref[s], 0, 0)),
                smem,
            ],
            out_specs=[
                pl.BlockSpec(
                    (part, per, 2, HS, HS),
                    lambda i, plan_ref, rot_ref: (lax.div(rot_ref[0], part) ^ i, 0, 0, 0, 0),
                ),
                pl.BlockSpec((step, rows, 2 * HS), lambda i, plan_ref, rot_ref: (i, 0, 0)),
            ],
        )
        return pl.pallas_call(
            functools.partial(maps_kernel, step, per),
            grid_spec=grid_spec,
            out_shape=[
                (pltpu.VMEM if UP_PERMUTE[s] else pltpu.HBM)((group, per, 2, HS, HS), F32),
                pltpu.HBM((heads, rows, 2 * HS), BF16),
            ],
            cost_estimate=cost(heads * 6 * rows * 256 * 256, heads * rows * HS * 12),
            compiler_params=limit(SMALL),
        )(plan, rots[UP_PERMUTE[s]], in_hbm(keys), in_hbm(values), in_hbm(token_gate), head_rate)

    def reads_of(s, errors):
        return pl.pallas_call(
            functools.partial(reads_kernel, step),
            grid_spec=pltpu.PrefetchScalarGridSpec(
                num_scalar_prefetch=1,
                grid=(heads // step,),
                in_specs=[seq_block(s), seq_block(s), gate_block(s), smem, t_block],
                out_specs=[col_block, col_block],
            ),
            out_shape=[
                pltpu.HBM((rows, width), BF16),
                pltpu.HBM((rows, width), BF16),
            ],
            cost_estimate=cost(heads * 8 * rows * 256 * 256, heads * rows * HS * 16),
            compiler_params=limit(SMALL),
        )(plan, in_hbm(queries), in_hbm(keys), in_hbm(token_gate), head_rate, in_hbm(errors))

    def one_of(parts_d, blocks):
        tail = (0,) * (len(blocks) - 1)
        if isinstance(parts_d, list):
            return parts_d, [pl.BlockSpec(blocks, lambda i, *_: (0,) + tail) for _ in parts_d]
        return [parts_d] * group, [pl.BlockSpec(blocks, lambda i, *_, d=d: (d,) + tail) for d in range(group)]

    start = lax.dynamic_slice_in_dim(init_state, place * per, per)

    def chain(s, gathered, moved, all_out, far):
        shape = (group, per, HS, HS) if all_out else (per, HS, HS)
        info = jnp.concatenate([rots[UP_PERMUTE[s]], block.reshape(1), rots[DOWN_PERMUTE[s]]])
        kind = "pieces" if isinstance(gathered, list) else "far" if far else "near"
        keeps = kind == "far" and not all_out
        hops = moved is not None
        given = [start, moved] if hops else [start]
        vmem, hbm = pl.BlockSpec(memory_space=pltpu.VMEM), pl.BlockSpec(memory_space=pltpu.HBM)
        given = [in_vmem(x) for x in given]
        specs = [smem] + [vmem] * len(given)
        pieces = gathered if kind == "pieces" else [gathered]
        given += [in_hbm(x) if kind == "far" else in_vmem(x) for x in pieces]
        specs += [hbm if kind == "far" else vmem] * len(pieces)
        streamed = all_out and not DOWN_PERMUTE[s]
        scratch = [] if kind == "near" or keeps else [pltpu.VMEM((group, per, 2, HS, HS), F32)]
        if kind == "far":
            scratch.append(pltpu.SemaphoreType.DMA((group,)))
        if streamed:
            scratch += [pltpu.VMEM(shape, F32), pltpu.SemaphoreType.DMA((group,))]
        return pl.pallas_call(
            functools.partial(chain_kernel, group, hops, all_out, kind, streamed),
            in_specs=specs,
            out_specs=[hbm if streamed else vmem] + [vmem] * keeps,
            scratch_shapes=scratch,
            out_shape=[pltpu.HBM(shape, F32) if streamed else jax.ShapeDtypeStruct(shape, F32)]
            + [pltpu.VMEM((group, per, 2, HS, HS), F32)] * keeps,
            compiler_params=limit(SMALL),
            cost_estimate=cost(group * per * 6 * HS**3, group * per * HS * HS * 12),
        )(info, *given)

    wide = WIDE if model % WIDE == 0 else model
    steps = heads // step

    def final_of(s, reads, entering):
        less, rest = reads
        piece = rows // parts
        early = lambda i: jnp.minimum(i, steps - 1)
        late = lambda i: jnp.maximum(i - steps, 0)
        by_cols = pl.BlockSpec((rows, step * HS), lambda i, *_: (0, early(i)))
        given, state_specs = one_of(entering, (1, per, HS, HS))
        return pl.pallas_call(
            functools.partial(final_kernel, steps, parts, group),
            grid_spec=pltpu.PrefetchScalarGridSpec(
                num_scalar_prefetch=3,
                grid=(steps + model // wide,),
                in_specs=[
                    pl.BlockSpec((1, rows, step * HS), lambda i, plan_ref, *_: (plan_ref[s], 0, early(i))),
                    by_cols,
                    by_cols,
                    pl.BlockSpec((1, step * HS), lambda i, *_: (0, early(i))),
                    pl.BlockSpec(memory_space=pltpu.HBM),
                ]
                + state_specs,
                out_specs=[pl.BlockSpec((piece, wide), lambda i, *_: (0, late(i)))] * parts,
                scratch_shapes=[
                    pltpu.VMEM((group, per, HS, HS), F32),
                    pltpu.VMEM((steps, rows, step * HS), BF16),
                    pltpu.VMEM((model // wide, steps, step * HS, wide), BF16),
                    pltpu.SemaphoreType.DMA((model // wide,)),
                ],
            ),
            compiler_params=limit(LARGE),
            out_shape=[(pltpu.HBM if s < seqs - 1 else pltpu.VMEM)((piece, model), F32)] * parts,
            cost_estimate=cost(2 * rows * width * model, 2 * width * model + 4 * rows * model),
        )(
            plan,
            me,
            rots[DOWN_PERMUTE[s]],
            in_hbm(queries),
            in_hbm(less),
            in_hbm(rest),
            in_hbm(norm_gain.reshape(1, width)),
            in_hbm(out_proj.reshape(steps, step * HS, model)),
            *map(in_vmem, given),
        )

    def shared(pieces, permute):
        if group == 1:
            return pieces
        if not permute:
            return lax.all_to_all(pieces, "ctx", 0, 0, tiled=True, axis_index_groups=groups)
        outs = [pieces[:1]]
        for d in range(1, group):
            outs.append(lax.ppermute(pieces[d : d + 1], "ctx", [(i, i ^ d) for i in range(ctx)]))
        return outs

    mapped = [maps_of(s) for s in range(seqs)]
    gathered = [shared(maps, UP_PERMUTE[s]) for s, (maps, _) in enumerate(mapped)]
    reads = [reads_of(s, errors) for s, (_, errors) in enumerate(mapped)]
    gathered[0], reads = lax.optimization_barrier((gathered[0], reads))
    outs = []
    for s in range(seqs):
        moved, held, far = None, gathered[s], s > 0
        for _ in range(ctx // group - 1):
            ending, *kept = chain(s, held, moved, False, far)
            held, far = (kept[0], False) if kept else (held, far)
            moved = lax.ppermute(ending, "ctx", onward)
        (leaving,) = chain(s, held, moved, True, far)
        entering = shared(leaving, DOWN_PERMUTE[s])
        products = final_of(s, reads[s], entering)
        outs.append(products[0])
        for d in range(1, parts):
            outs.append(lax.ppermute(products[d], "head", [(i, i ^ d) for i in range(parts)]))
    piece = rows // parts
    wider = 2048 if model % 2048 == 0 else model
    return pl.pallas_call(
        functools.partial(sum_kernel, parts),
        grid=(model // wider,),
        in_specs=[pl.BlockSpec((piece, wider), lambda i: (0, i))] * len(outs),
        out_specs=pl.BlockSpec((piece, seqs, wider), lambda i: (0, 0, i)),
        out_shape=jax.ShapeDtypeStruct((piece, seqs, model), BF16),
        compiler_params=limit(2 * SMALL),
        cost_estimate=cost(2 * (piece * seqs) ** 2 * model, 4 * len(outs) * piece * model),
        name="sums",
    )(*outs)


def solution(mesh):
    return jax.shard_map(
        per_device,
        mesh=mesh,
        in_specs=(
            P(None, "ctx", "head"),
            P(None, "ctx", "head"),
            P(None, "ctx", "head"),
            P(None, "head", "ctx"),
            P("head"),
            P("head", None, None),
            P("head"),
            P("head", None),
            P(),
        ),
        out_specs=P(("ctx", "head"), None, None),
        check_vma=False,
    )
```
